32 devices in a mesh: cluster: 4 (over z), tm: 8 (over y, x, core).
Axes of the slice: x: 2, y: 2, z: 4, core: 2. Of those that a mesh axis runs over, the one named last changes fastest.
Arguments:
- obs: float32 [12, 512, 128], P('cluster', 'tm'), parts along dimension 0, may hold values from -6 to 6
- present: int32 [12, 512], P('cluster', 'tm'), parts along dimension 0, may hold values 0 or 1
- sensors: int32 [4], P('cluster'), parts along dimension 0, may hold values from 32 to 128
- log_prec: float32 [512], P('cluster'), parts along dimension 0, may hold values from -1 to 1
- dynamics: float32 [512, 128], P('cluster'), parts along dimension 0, may hold values from -1 to 1
- prior_var: float32 [512], P('cluster'), parts along dimension 0, may hold values from 0 to 0.06, as said below
- obs_map: float32 [512, 128], P('cluster'), parts along dimension 0, may hold values from -0.5 to 0.5
- init_state: float32 [12, 128], P('cluster'), parts along dimension 0, may hold values from -6 to 6
Outputs:
- smoothed: float32 [12, 512, 128], P('cluster', 'tm'), parts along dimension 0
- new_log_prec: float32 [512], P('cluster'), parts along dimension 0
- mean_loglik: float32 [4], P('cluster'), parts along dimension 0
The draws below stay inside these ranges and needn't reach their ends.
There are 4 independent parts, one for each index of `cluster`. The reference program is written for one: setup_inputs(seed, part) draws one part's arguments, and reference() takes and returns one part's arrays. A program takes and returns all parts, laid end to end along the dimension named above; each array names one. Nothing has to cross between parts.
Inputs may be any that keep to these rules, and one draw needn't show every extreme that they name: `prior_var`: positive variances.
All inputs are finite; a program needn't handle non-finite values. No bound on the sum of `present` on one device may be relied on, other than what follows from the above.
Results may differ from the reference program's by a relative error of at most 0.0003.
Values sent between devices are 32-bit elements; how exact they have to be, the bound alone decides.
A program may use at most 128 MiB of HBM per device.

```python
import math
import jax
import jax.numpy as jnp
from jax import lax

S = 128
P_SIZE = 128
SEQS = 3
STEPS = 512


def structure(key):
    folded = jax.random.fold_in(key, 31)
    subkeys = jax.random.split(folded, 4)
    share = 0.5
    slow_mask = jax.random.uniform(subkeys[0], (S,)) < share
    slow_rate = jnp.exp(jnp.log(0.3) / STEPS)
    memory_steps = jax.random.uniform(subkeys[1], (S,), minval=30.0, maxval=50.0)
    decay_rates = jnp.where(slow_mask, slow_rate, jnp.exp(-1.0 / memory_steps))
    same_group = (slow_mask[:, None] == slow_mask[None, :]).astype(jnp.float32)
    mixing_noise = jax.random.normal(subkeys[2], (S, S)) * (0.35 / math.sqrt(S))
    initial = (jnp.eye(S, dtype=jnp.float32) + mixing_noise * same_group) / 1.8

    def refine(repeat, matrix):
        cubic = jnp.dot(jnp.dot(matrix, matrix.T, precision=lax.Precision.HIGHEST), matrix, precision=lax.Precision.HIGHEST)
        return 1.5 * matrix - 0.5 * cubic
    rotation = lax.fori_loop(0, 40, refine, initial)
    transition = decay_rates[:, None] * rotation
    variances = jnp.where(slow_mask, 0.3 / STEPS, 0.05) * jax.random.uniform(subkeys[3], (S,), minval=0.9, maxval=1.1)
    return (transition.astype(jnp.float32), variances.astype(jnp.float32))


def draw_dynamics(key, part):
    return structure(key)[0]


def draw_prior_var(key, part):
    return structure(key)[1]


def set_ends(entries, key, smallest, high):
    dims = entries.shape
    place = [jax.random.randint(jax.random.fold_in(key, axis), (), 0, dims[axis]) for axis in range(len(dims))]
    entries = entries.at[tuple(place)].set(smallest)
    longest = dims.index(max(dims))
    place[longest] = (place[longest] + 1) % dims[longest]
    return entries.at[tuple(place)].set(high)


def steps_of(own_key, dims, shards, least, high):
    def one(position, shards_of):
        steps = jax.random.uniform(jax.random.fold_in(jax.random.fold_in(own_key, 6), position), (shards_of,), jnp.float32, least / len(shards), high / len(shards))
        return jnp.repeat(jnp.exp(steps), dims[position] // shards_of).reshape((-1,) + (1,) * (len(dims) - position - 1))

    level = one(*shards[0])
    for cut in shards[1:]:
        level = level * one(*cut)
    return level


def normal_values(rng, shape, spread, bound, cuts=(), held_as=jnp.bfloat16):
    entries = jax.random.normal(rng, shape, jnp.float32) * spread
    if len(cuts) > 0:
        entries = steps_of(rng, shape, cuts, -0.22, 0.18) * entries
    return jnp.clip(entries, min=-bound, max=bound).astype(held_as)


def setup_inputs(seed: int = 0, part: int = 0) -> dict:
    splits = jax.random.split(jax.random.key(seed), 9)
    own_keys = jax.random.split(jax.random.fold_in(splits[8], part), 9)
    obs = normal_values(own_keys[0], (SEQS, STEPS, P_SIZE), 1.0, 6.0, ((1, 8),), jnp.float32)
    present = set_ends((jax.random.randint(own_keys[1], (SEQS, STEPS), 0, 5) < 4).astype(jnp.int32), jax.random.fold_in(own_keys[1], 1), 0, 1)
    sensors = jax.random.randint(own_keys[2], (1,), P_SIZE // 4, P_SIZE + 1).astype(jnp.int32)
    log_prec = jnp.clip(jax.random.uniform(own_keys[3], (P_SIZE,), jnp.float32, -1.0, 1.0), -1.0, 1.0)
    dynamics = draw_dynamics(jax.random.fold_in(jax.random.fold_in(splits[8], part), 71), part)
    prior_var = draw_prior_var(jax.random.fold_in(jax.random.fold_in(splits[8], part), 71), part)
    obs_map = normal_values(own_keys[6], (P_SIZE, S), S ** -0.5, 0.5, (), jnp.float32)
    init_state = normal_values(own_keys[7], (SEQS, S), 1.0, 6.0, (), jnp.float32)
    return dict(obs=obs, present=present, sensors=sensors, log_prec=log_prec, dynamics=dynamics, prior_var=prior_var, obs_map=obs_map, init_state=init_state)


def reference(obs, present, sensors, log_prec, dynamics, prior_var, obs_map, init_state):
    highest = lax.Precision.HIGHEST
    channel_on = (jnp.arange(P_SIZE) < sensors[0]).astype(jnp.float32)
    sensor_precision = jnp.exp(log_prec)
    gain_matrix = prior_var[:, None] * (obs_map.T * (sensor_precision * channel_on)[None, :])
    outputs = []
    gradient = jnp.zeros((P_SIZE,), jnp.float32)
    loglik = jnp.zeros((), jnp.float32)
    for sequence in range(SEQS):
        def forward(carried, inputs):
            reading, flag = inputs
            predicted = jnp.dot(dynamics, carried, precision=highest)
            innovation = channel_on * (reading - jnp.dot(obs_map, predicted, precision=highest))
            updated = predicted + flag.astype(jnp.float32) * jnp.dot(gain_matrix, innovation, precision=highest)
            return updated, (updated, innovation)

        last_state, (filtered, innovations) = lax.scan(forward, init_state[sequence], (obs[sequence], present[sequence]))

        def backward(later, current):
            moved = later - jnp.dot(dynamics, current, precision=highest)
            smooth = current + jnp.dot(dynamics.T, moved, precision=highest)
            return smooth, smooth

        boundary = jnp.dot(dynamics, last_state, precision=highest)
        ignored, smooth_states = lax.scan(backward, boundary, filtered, reverse=True)
        outputs.append(smooth_states)
        observed = present[sequence].astype(jnp.float32)[:, None]
        weighted = sensor_precision * innovations * innovations
        gradient = gradient + 0.5 * jnp.sum(observed * channel_on * (1.0 - weighted), axis=0)
        loglik = loglik + 0.5 * jnp.sum(observed * channel_on * (log_prec - weighted))
    count_all = SEQS * STEPS
    smoothed = jnp.stack(outputs)
    new_log_prec = log_prec + gradient / count_all
    mean_loglik = (loglik / (count_all * P_SIZE)).reshape(1)
    return smoothed, new_log_prec, mean_loglik
```

```python
import functools
import math

import jax
import jax.numpy as jnp
from jax import lax
from jax.experimental import pallas as pl
from jax.experimental.pallas import tpu as pltpu
from jax.sharding import PartitionSpec as P

F32 = jnp.float32
BF16 = jnp.bfloat16
MESH = pl.DeviceIdType.MESH
WORD = 4


def stacked(a):
    high = a.astype(BF16).astype(F32)
    return jnp.concatenate([high, a - high], axis=0).astype(BF16)


def twice(s):
    return jnp.concatenate([s, s], axis=1)


def product(left, right):
    full = jnp.dot(left, right, preferred_element_type=F32)
    rows = full.shape[0] // 2
    return full[:rows] + full[rows:]


def times(a, right):
    return product(twice(stacked(a)), right)


def over(count, width, body):
    if count <= width:
        for i in range(count):
            body(i)
        return
    assert count % width == 0

    def step(lap, _):
        for i in range(width):
            body(lap * width + i)
        return 0

    lax.fori_loop(0, count // width, step, 0)


def kernel(
    n, seqs, steps,
    present_s, sensors_s, obs, present_v, log_prec, dyn, prior_var, obs_map, init,
    out, new_prec, loglik,
    words, table, nodes, vecs, ents, pair_rhs, step_rhs, drive, mask, offs, prior, filt,
    suffix, chunk8, in_buf, out_buf, off_buf, off_in, sum_buf, sum_in,
    chain_sem, off_send, off_recv, sum_send, sum_recv,
):
    pos = lax.axis_index("tm")
    states = dyn.shape[0]
    chunks = steps // WORD
    total = seqs * chunks
    levels = int(math.log2(chunks))
    first = [0]
    for level in range(1, levels + 1):
        first.append(first[-1] + (total >> (level - 1) if level > 1 else 0))

    in_buf[...] = jnp.zeros_like(in_buf)
    off_in[...] = jnp.zeros_like(off_in)
    barrier = pltpu.get_barrier_semaphore()
    for d in range(1, n):
        pl.semaphore_signal(barrier, inc=1, device_id={"tm": lax.rem(pos + d, n)}, device_id_type=MESH)

    lane = lax.broadcasted_iota(jnp.int32, (1, states), 1)
    active = (lane < sensors_s[0]).astype(F32)
    weight = jnp.exp(log_prec[...])
    weight_on = weight * active
    pv = prior_var[...]
    d_mat = dyn[...]
    d_t = d_mat.T
    h_mat = obs_map[...]
    h_rhs = stacked(h_mat)
    d_rhs = stacked(d_mat)
    readout = times(h_mat, d_rhs).T
    f_t = d_t - times(readout * weight_on, h_rhs) * pv

    for b in range(seqs):
        def word(k, b=b):
            t = k * WORD
            w = present_s[b, t]
            for i in range(1, WORD):
                w = w * 2 + present_s[b, t + i]
            words[b * chunks + k] = w
        over(chunks, 16, word)
        row = jnp.broadcast_to(present_v[b : b + 1, :].astype(F32), (steps, steps))
        same = lax.broadcasted_iota(jnp.int32, (steps, steps), 0) == lax.broadcasted_iota(jnp.int32, (steps, steps), 1)
        column = jnp.sum(jnp.where(same, row, 0.0), axis=1, keepdims=True)
        mask[b * steps : (b + 1) * steps, :] = jnp.broadcast_to(column, (steps, states))

    drive[...] = times(obs[...] * weight_on, h_rhs) * pv * mask[...]

    both = jnp.concatenate([d_t, f_t], axis=1)
    step_rhs[...] = stacked(both)
    pairs = []
    for a in (d_t, f_t):
        pairs.append(times(a, step_rhs[...]))
    pair_rhs[...] = stacked(jnp.concatenate(pairs, axis=1))
    for a in range(4):
        rows = pairs[a // 2][:, (a % 2) * states : (a % 2 + 1) * states]
        quad = times(rows, pair_rhs[...])
        for c in range(4):
            table[a * 4 + c] = stacked(quad[:, c * states : (c + 1) * states])

    def at(ref, i):
        return ref[pl.ds(i, total, stride=WORD), :]

    def advance(x, i):
        y = times(x, step_rhs[...])
        return jnp.where(at(mask, i) > 0.5, y[:, states:], y[:, :states]) + at(drive, i)

    x = at(drive, 0)
    for i in range(1, WORD):
        x = advance(x, i)
    offs[...] = x

    eye = (
        lax.broadcasted_iota(jnp.int32, (states, states), 0)
        == lax.broadcasted_iota(jnp.int32, (states, states), 1)
    ).astype(F32)
    residual = eye - jnp.dot(d_t, d_mat, precision=lax.Precision.HIGHEST, preferred_element_type=F32)
    by_one = times(jnp.concatenate([residual, d_mat], axis=0), d_rhs)
    r_1, d_2 = by_one[:states], by_one[states:]
    by_two = times(jnp.concatenate([residual, r_1, d_mat, d_2], axis=0), stacked(d_2))
    r_2, r_3 = by_two[:states], by_two[states : 2 * states]
    d_3, d_4 = by_two[2 * states : 3 * states], by_two[3 * states :]
    tail_rhs = stacked(jnp.concatenate([residual, r_1, r_2, r_3], axis=1))
    fill_rhs = stacked(jnp.concatenate([d_4, d_3, d_2, d_mat], axis=1))
    power = stacked(d_4)
    powers = [power]

    for level in range(1, levels + 1):
        base, below = first[level], first[level - 1]

        def compose(j, level=level, base=base, below=below):
            if level == 1:
                left, right = table[words[2 * j]], table[words[2 * j + 1]]
                v_left, v_right = offs[pl.ds(2 * j, 1), :], offs[pl.ds(2 * j + 1, 1), :]
            else:
                left, right = nodes[below + 2 * j], nodes[below + 2 * j + 1]
                v_left, v_right = vecs[pl.ds(below + 2 * j, 1), :], vecs[pl.ds(below + 2 * j + 1, 1), :]
            rows = jnp.concatenate([left, stacked(jnp.broadcast_to(v_left, (8, states)))], axis=0)
            y = jnp.dot(twice(rows), right, preferred_element_type=F32)
            nodes[base + j] = stacked(y[:states] + y[states : 2 * states])
            vecs[pl.ds(base + j, 1), :] = (
                y[2 * states : 2 * states + 1] + y[2 * states + 8 : 2 * states + 9] + v_right
            )

        over(total >> level, 6, compose)
        power = stacked(product(twice(powers[-1]), powers[-1]))
        powers.append(power)
    laps = []
    for _ in range(int(math.log2(n))):
        laps.append(power)
        power = stacked(product(twice(power), power))

    pl.semaphore_wait(barrier, n - 1)
    row8 = lax.broadcasted_iota(jnp.int32, (8, states), 0)

    chain = pltpu.make_async_remote_copy(
        src_ref=out_buf, dst_ref=in_buf, send_sem=chain_sem.at[0], recv_sem=chain_sem.at[1],
        device_id={"tm": lax.rem(pos + 1, n)}, device_id_type=MESH,
    )

    @pl.when(pos == 0)
    def _():
        in_buf[0:seqs, :] = init[...]

    @pl.when(pos > 0)
    def _():
        chain.wait_recv()

    entering = in_buf[...]
    top = first[levels]
    left = twice(stacked(entering))

    @pl.when(pos < n - 1)
    def _():
        leaving = jnp.zeros((8, states), F32)
        for b in range(seqs):
            y = product(left, nodes[top + b]) + vecs[top + b : top + b + 1, :]
            leaving = jnp.where(row8 == b, y, leaving)
        out_buf[...] = leaving
        chain.start()

    e_first = [0]
    for level in range(levels, 0, -1):
        e_first.append(e_first[-1] + (((total >> level) + 7) // 8) * 8)
    ents[0:seqs, :] = entering[0:seqs]
    for lap, level in enumerate(range(levels, 0, -1)):
        source, target, below = e_first[lap], e_first[lap + 1], first[level - 1]

        def descend(j, level=level, source=source, target=target, below=below):
            e = ents[pl.ds(source + j, 1), :]
            if level == 1:
                mat, v = table[words[2 * j]], offs[pl.ds(2 * j, 1), :]
            else:
                mat, v = nodes[below + 2 * j], vecs[pl.ds(below + 2 * j, 1), :]
            y = times(jnp.broadcast_to(e, (8, states)), mat)
            ents[pl.ds(target + 2 * j, 1), :] = e
            ents[pl.ds(target + 2 * j + 1, 1), :] = y[0:1] + v

        over(total >> level, 6, descend)

    x = ents[pl.ds(e_first[-1], total), :]
    for i in range(WORD):
        prior[i * total : (i + 1) * total, :] = x
        x = advance(x, i)
        filt[i * total : (i + 1) * total, :] = x

    y = times(filt[...], tail_rhs)

    def part(i, k):
        return y[i * total : (i + 1) * total, k * states : (k + 1) * states]

    chunk8[...] = jnp.zeros_like(chunk8)
    for i in range(WORD):
        z = part(i, 0)
        for j in range(i + 1, WORD):
            z = z + part(j, j - i)
        suffix[i * total : (i + 1) * total, :] = z
        if i == 0:
            for b in range(seqs):
                chunk8[pl.ds(b, chunks, stride=8), :] = z[b * chunks : (b + 1) * chunks]

    ups = [chunk8[...].reshape(chunks, 8, states)]
    for level in range(levels):
        pair = ups[-1].reshape(ups[-1].shape[0] // 2, 2, 8, states)
        half = pair.shape[0]
        later = times(pair[:, 1].reshape(half * 8, states), powers[level])
        ups.append(pair[:, 0] + later.reshape(half, 8, states))

    last = jnp.zeros((8, states), F32)
    for b in range(seqs):
        r = (WORD - 1) * total + (b + 1) * chunks - 1
        last = jnp.where(row8 == b, jnp.broadcast_to(filt[r : r + 1, :], (8, states)), last)
    final = times(last, stacked(d_t))
    own = ups[-1][0] + jnp.where(pos == n - 1, times(final, powers[levels]), 0.0)
    off_buf[...] = own

    def send_off(d):
        return pltpu.make_async_remote_copy(
            src_ref=off_buf, dst_ref=off_in.at[d], send_sem=off_send.at[d], recv_sem=off_recv.at[d],
            device_id={"tm": lax.rem(pos + n - 1 - d, n)}, device_id_type=MESH,
        )

    for d in range(n - 1):
        @pl.when(pos - 1 - d >= 0)
        def _(d=d):
            send_off(d).start()

    obs_rows = [at(obs, i) for i in range(WORD)]
    mask_rows = [at(mask, i) for i in range(WORD)]
    errors = jnp.concatenate(obs_rows, axis=0) - times(prior[...], stacked(readout))
    seen = jnp.concatenate(mask_rows, axis=0)
    squares = jnp.sum(seen * active * errors * errors, axis=0, keepdims=True)
    number = jnp.sum(seen, axis=0, keepdims=True)
    sums = jnp.where(row8 == 0, jnp.broadcast_to(squares, (8, states)), jnp.broadcast_to(number, (8, states)))
    sum_buf[...] = sums

    def send_sum(d):
        return pltpu.make_async_remote_copy(
            src_ref=sum_buf, dst_ref=sum_in.at[d], send_sem=sum_send.at[d], recv_sem=sum_recv.at[d],
            device_id={"tm": lax.rem(pos + d + 1, n)}, device_id_type=MESH,
        )

    for d in range(n - 1):
        send_sum(d).start()

    for d in range(n - 1):
        @pl.when(pos + 1 + d < n)
        def _(d=d):
            send_off(d).wait_recv()

    x = off_in[...]
    for power in laps:
        pair = x.reshape(x.shape[0] // 2, 2, 8, states)
        half = pair.shape[0]
        x = pair[:, 0] + times(pair[:, 1].reshape(half * 8, states), power).reshape(half, 8, states)
    x = jnp.where(pos == n - 1, final, x[0])[None]
    for level in range(levels - 1, -1, -1):
        count = x.shape[0]
        pair = ups[level].reshape(count, 2, 8, states)
        early = times(x.reshape(count * 8, states), powers[level]).reshape(count, 8, states) + pair[:, 1]
        x = jnp.stack([early, x], axis=1).reshape(2 * count, 8, states)
    chunk8[...] = x.reshape(chunks * 8, states)
    x = jnp.concatenate([chunk8[pl.ds(b, chunks, stride=8), :] for b in range(seqs)], axis=0)
    y = times(x, fill_rhs)
    for i in range(WORD):
        out[pl.ds(i, total, stride=WORD), :] = (
            suffix[i * total : (i + 1) * total, :] + y[:, i * states : (i + 1) * states]
        )

    for d in range(n - 1):
        send_sum(d).wait_recv()
        sums = sums + sum_in[d]
    squares, number = sums[0:1], sums[1:2]
    grad = 0.5 * active * (number - weight * squares)
    new_prec[...] = log_prec[...] + grad / (seqs * steps * n)
    terms = 0.5 * active * (log_prec[...] * number - weight * squares)
    loglik[...] = jnp.sum(terms, axis=1, keepdims=True) / (seqs * steps * n * states)

    @pl.when(pos < n - 1)
    def _():
        chain.wait_send()

    for d in range(n - 1):
        @pl.when(pos - 1 - d >= 0)
        def _(d=d):
            send_off(d).wait_send()
        send_sum(d).wait_send()


def local(n, obs, present, sensors, log_prec, dynamics, prior_var, obs_map, init_state):
    seqs, steps, channels = obs.shape
    states = dynamics.shape[0]
    chunks = steps // WORD
    total = seqs * chunks
    inner = sum(total >> level for level in range(1, int(math.log2(chunks)) + 1))
    ents = sum((((total >> level) + 7) // 8) * 8 for level in range(0, int(math.log2(chunks)) + 1))
    vmem = pl.BlockSpec(memory_space=pltpu.VMEM)
    smem = pl.BlockSpec(memory_space=pltpu.SMEM)
    rows = seqs * steps
    smoothed, new_prec, loglik = pl.pallas_call(
        functools.partial(kernel, n, seqs, steps),
        out_shape=(
            jax.ShapeDtypeStruct((rows, states), F32),
            jax.ShapeDtypeStruct((1, channels), F32),
            jax.ShapeDtypeStruct((1, 1), F32),
        ),
        in_specs=[smem, smem] + [vmem] * 7,
        out_specs=(vmem, vmem, vmem),
        scratch_shapes=[
            pltpu.SMEM((total,), jnp.int32),
            pltpu.VMEM((2**WORD, 2 * states, states), BF16),
            pltpu.VMEM((inner, 2 * states, states), BF16),
            pltpu.VMEM(((inner + 7) // 8 * 8, states), F32),
            pltpu.VMEM((ents, states), F32),
            pltpu.VMEM((2 * states, 4 * states), BF16),
            pltpu.VMEM((2 * states, 2 * states), BF16),
            pltpu.VMEM((rows, states), F32),
            pltpu.VMEM((rows, states), F32),
            pltpu.VMEM((total, states), F32),
            pltpu.VMEM((rows, states), F32),
            pltpu.VMEM((rows, states), F32),
            pltpu.VMEM((rows, states), F32),
            pltpu.VMEM((chunks * 8, states), F32),
            pltpu.VMEM((8, states), F32),
            pltpu.VMEM((8, states), F32),
            pltpu.VMEM((8, states), F32),
            pltpu.VMEM((n, 8, states), F32),
            pltpu.VMEM((8, states), F32),
            pltpu.VMEM((n, 8, states), F32),
            pltpu.SemaphoreType.DMA((2,)),
            pltpu.SemaphoreType.DMA((n,)),
            pltpu.SemaphoreType.DMA((n,)),
            pltpu.SemaphoreType.DMA((n,)),
            pltpu.SemaphoreType.DMA((n,)),
        ],
        compiler_params=pltpu.CompilerParams(collective_id=0, has_side_effects=True),
        name="kalman",
    )(
        present, sensors, obs.reshape(rows, channels), present, log_prec.reshape(1, channels),
        dynamics, prior_var.reshape(1, states), obs_map, init_state,
    )
    return smoothed.reshape(seqs, steps, states), new_prec.reshape(channels), loglik.reshape(1)


def solution(mesh):
    in_specs = (
        P("cluster", "tm", None),
        P("cluster", "tm"),
        P("cluster"),
        P("cluster"),
        P("cluster", None),
        P("cluster"),
        P("cluster", None),
        P("cluster", None),
    )
    out_specs = (P("cluster", "tm", None), P("cluster"), P("cluster"))
    body = functools.partial(local, mesh.shape["tm"])
    return jax.shard_map(body, mesh=mesh, in_specs=in_specs, out_specs=out_specs, check_vma=False)
```

```python
import functools
import math

import jax
import jax.numpy as jnp
from jax import lax
from jax.experimental import pallas as pl
from jax.experimental.pallas import tpu as pltpu
from jax.sharding import PartitionSpec as P

F32 = jnp.float32
BF16 = jnp.bfloat16
MESH = pl.DeviceIdType.MESH
WORD = 4


def stacked(a):
    high = a.astype(BF16).astype(F32)
    return jnp.concatenate([high, a - high], axis=0).astype(BF16)


def twice(s):
    return jnp.concatenate([s, s], axis=1)


def product(left, right):
    full = jnp.dot(left, right, preferred_element_type=F32)
    rows = full.shape[0] // 2
    return full[:rows] + full[rows:]


def times(a, right):
    return product(twice(stacked(a)), right)


def over(count, width, body):
    if count <= width:
        for i in range(count):
            body(i)
        return
    assert count % width == 0

    def step(lap, _):
        for i in range(width):
            body(lap * width + i)
        return 0

    lax.fori_loop(0, count // width, step, 0)


def kernel(
    n, seqs, steps,
    present_s, sensors_s, obs, present_v, log_prec, dyn, prior_var, obs_map, init,
    out, new_prec, loglik,
    words, table, nodes, vecs, ents, heads, head_vecs, power_rows, power_cols, lap_rhs, pair_rhs, step_rhs, drive, mask, offs, prior, filt,
    suffix, chunk8, in_buf, out_buf, off_buf, off_in, sum_buf, sum_in,
    chain_sem, off_send, off_recv, sum_send, sum_recv,
):
    pos = lax.axis_index("tm")
    states = dyn.shape[0]
    chunks = steps // WORD
    total = seqs * chunks
    levels = int(math.log2(chunks))
    first = [0]
    for level in range(1, levels + 1):
        first.append(first[-1] + (total >> (level - 1) if level > 1 else 0))

    in_buf[...] = jnp.zeros_like(in_buf)
    off_in[...] = jnp.zeros_like(off_in)
    barrier = pltpu.get_barrier_semaphore()
    for d in range(1, n):
        pl.semaphore_signal(barrier, inc=1, device_id={"tm": lax.rem(pos + d, n)}, device_id_type=MESH)

    lane = lax.broadcasted_iota(jnp.int32, (1, states), 1)
    active = (lane < sensors_s[0]).astype(F32)
    weight = jnp.exp(log_prec[...])
    weight_on = weight * active
    pv = prior_var[...]
    d_mat = dyn[...]
    d_t = d_mat.T
    h_mat = obs_map[...]
    h_rhs = stacked(h_mat)
    d_rhs = stacked(d_mat)
    readout = times(h_mat, d_rhs).T
    f_t = d_t - times(readout * weight_on, h_rhs) * pv

    for b in range(seqs):
        def word(k, b=b):
            t = k * WORD
            w = present_s[b, t]
            for i in range(1, WORD):
                w = w * 2 + present_s[b, t + i]
            words[b * chunks + k] = w
        over(chunks, 16, word)
        row = jnp.broadcast_to(present_v[b : b + 1, :].astype(F32), (steps, steps))
        same = lax.broadcasted_iota(jnp.int32, (steps, steps), 0) == lax.broadcasted_iota(jnp.int32, (steps, steps), 1)
        column = jnp.sum(jnp.where(same, row, 0.0), axis=1, keepdims=True)
        mask[b * steps : (b + 1) * steps, :] = jnp.broadcast_to(column, (steps, states))

    drive[...] = times(obs[...] * weight_on, h_rhs) * pv * mask[...]

    both = jnp.concatenate([d_t, f_t], axis=1)
    step_rhs[...] = stacked(both)
    pairs = []
    for a in (d_t, f_t):
        pairs.append(times(a, step_rhs[...]))
    pair_rhs[...] = stacked(jnp.concatenate(pairs, axis=1))
    for a in range(4):
        rows = pairs[a // 2][:, (a % 2) * states : (a % 2 + 1) * states]
        quad = times(rows, pair_rhs[...])
        for c in range(4):
            table[a * 4 + c] = stacked(quad[:, c * states : (c + 1) * states])

    def at(ref, i):
        return ref[pl.ds(i, total, stride=WORD), :]

    def advance(x, i):
        y = times(x, step_rhs[...])
        return jnp.where(at(mask, i) > 0.5, y[:, states:], y[:, :states]) + at(drive, i)

    x = at(drive, 0)
    for i in range(1, WORD):
        x = advance(x, i)
    offs[...] = x

    eye = (
        lax.broadcasted_iota(jnp.int32, (states, states), 0)
        == lax.broadcasted_iota(jnp.int32, (states, states), 1)
    ).astype(F32)
    residual = eye - times(d_t, d_rhs)
    by_one = times(jnp.concatenate([residual, d_mat], axis=0), d_rhs)
    r_1, d_2 = by_one[:states], by_one[states:]
    by_two = times(jnp.concatenate([residual, r_1, d_mat, d_2], axis=0), stacked(d_2))
    r_2, r_3 = by_two[:states], by_two[states : 2 * states]
    d_3, d_4 = by_two[2 * states : 3 * states], by_two[3 * states :]
    tail_rhs = stacked(jnp.concatenate([residual, r_1, r_2, r_3], axis=1))
    fill_rhs = stacked(jnp.concatenate([d_4, d_3, d_2, d_mat], axis=1))

    def keep_power(e, stack):
        if e < chunks:
            power_rows[e * 2 * states : (e + 1) * 2 * states, :] = stack
            power_cols[:, (chunks - 1 - e) * states : (chunks - e) * states] = stack
        else:
            lap_rhs[0 : 2 * states, :] = stack

    def power_of(e):
        return power_rows[e * 2 * states : (e + 1) * 2 * states, :]

    keep_power(0, stacked(eye))
    keep_power(1, stacked(d_4))

    for level in range(1, levels + 1):
        base, below = first[level], first[level - 1]

        def compose(j, level=level, base=base, below=below):
            if level == 1:
                left, right = table[words[2 * j]], table[words[2 * j + 1]]
                v_left, v_right = offs[pl.ds(2 * j, 1), :], offs[pl.ds(2 * j + 1, 1), :]
            else:
                left, right = nodes[below + 2 * j], nodes[below + 2 * j + 1]
                v_left, v_right = vecs[pl.ds(below + 2 * j, 1), :], vecs[pl.ds(below + 2 * j + 1, 1), :]
            rows = jnp.concatenate([left, stacked(jnp.broadcast_to(v_left, (8, states)))], axis=0)
            y = jnp.dot(twice(rows), right, preferred_element_type=F32)
            nodes[base + j] = stacked(y[:states] + y[states : 2 * states])
            vecs[pl.ds(base + j, 1), :] = (
                y[2 * states : 2 * states + 1] + y[2 * states + 8 : 2 * states + 9] + v_right
            )

        over(total >> level, total, compose)
        half = power_of(1 << (level - 1))
        keep_power(1 << level, stacked(product(twice(half), half)))

    def prepare():
        for b in range(seqs):
            rows = slice(b * 2 * states, (b + 1) * 2 * states)
            heads[rows, 0:states] = stacked(eye)
            for level in range(levels, 0, -1):
                for p in range(chunks >> level):
                    j = b * (chunks >> (level - 1)) + 2 * p
                    k = (p << level) + (1 << (level - 1))
                    if level == 1:
                        mat, v = table[words[j]], offs[j : j + 1, :]
                    else:
                        j = first[level - 1] + j
                        mat, v = nodes[j], vecs[j : j + 1, :]
                    if p > 0:
                        before = p << level
                        e_rows = head_vecs[b * chunks + before : b * chunks + before + 1, :]
                        left = jnp.concatenate(
                            [heads[rows, before * states : (before + 1) * states],
                             stacked(jnp.broadcast_to(e_rows, (8, states)))], axis=0)
                        y = jnp.dot(twice(left), mat, preferred_element_type=F32)
                        mat = stacked(y[:states] + y[states : 2 * states])
                        v = y[2 * states : 2 * states + 1] + y[2 * states + 8 : 2 * states + 9] + v
                    heads[rows, k * states : (k + 1) * states] = mat
                    head_vecs[b * chunks + k : b * chunks + k + 1, :] = v
        for level in range(1, levels):
            base = power_of(1 << level)
            for e in range(1, 1 << level):
                keep_power((1 << level) + e, stacked(product(twice(power_of(e)), base)))
        for d in range(1, n - 2):
            half = (d + 1) // 2 - 1
            other = d - 1 - half
            lap_rhs[d * 2 * states : (d + 1) * 2 * states, :] = stacked(
                product(
                    twice(lap_rhs[half * 2 * states : (half + 1) * 2 * states, :]),
                    lap_rhs[other * 2 * states : (other + 1) * 2 * states, :],
                )
            )

    head_vecs[...] = jnp.zeros_like(head_vecs)
    early = n // 2

    @pl.when(pos >= early)
    def _():
        prepare()

    pl.semaphore_wait(barrier, n - 1)
    row8 = lax.broadcasted_iota(jnp.int32, (8, states), 0)

    chain = pltpu.make_async_remote_copy(
        src_ref=out_buf, dst_ref=in_buf, send_sem=chain_sem.at[0], recv_sem=chain_sem.at[1],
        device_id={"tm": lax.rem(pos + 1, n)}, device_id_type=MESH,
    )

    @pl.when(pos == 0)
    def _():
        in_buf[0:seqs, :] = init[...]

    @pl.when(pos > 0)
    def _():
        chain.wait_recv()

    entering = in_buf[...]
    top = first[levels]
    left = jnp.concatenate(
        [twice(stacked(jnp.where(row8 == b, entering, 0.0))) for b in range(seqs)], axis=1
    )

    @pl.when(pos < n - 1)
    def _():
        leaving = product(left, nodes[top : top + seqs].reshape(seqs * 2 * states, states))
        for b in range(seqs):
            leaving = leaving + jnp.where(row8 == b, vecs[top + b : top + b + 1, :], 0.0)
        out_buf[...] = leaving
        chain.start()

    @pl.when(pos < early)
    def _():
        prepare()

    y = product(left, heads[...])
    for k in range(chunks):
        ents[pl.ds(k, seqs, stride=chunks), :] = y[0:seqs, k * states : (k + 1) * states]
    x = ents[...] + head_vecs[...]
    for i in range(WORD):
        prior[i * total : (i + 1) * total, :] = x
        x = advance(x, i)
        filt[i * total : (i + 1) * total, :] = x

    y = times(filt[...], tail_rhs)

    def part(i, k):
        return y[i * total : (i + 1) * total, k * states : (k + 1) * states]

    chunk8[...] = jnp.zeros_like(chunk8)
    for i in range(WORD):
        z = part(i, 0)
        for j in range(i + 1, WORD):
            z = z + part(j, j - i)
        suffix[i * total : (i + 1) * total, :] = z
        if i == 0:
            for b in range(seqs):
                chunk8[pl.ds(b, chunks, stride=8), :] = z[b * chunks : (b + 1) * chunks]

    last = jnp.zeros((8, states), F32)
    for b in range(seqs):
        r = (WORD - 1) * total + (b + 1) * chunks - 1
        last = jnp.where(row8 == b, jnp.broadcast_to(filt[r : r + 1, :], (8, states)), last)
    final = times(last, stacked(d_t))
    ends = chunk8[...].reshape(chunks, 8, states)
    left = jnp.concatenate([twice(stacked(ends[k])) for k in range(chunks)], axis=1)
    own = product(left, power_rows[...])
    own = own + jnp.where(pos == n - 1, times(final, lap_rhs[0 : 2 * states, :]), 0.0)
    off_buf[...] = own

    def send_off(d):
        return pltpu.make_async_remote_copy(
            src_ref=off_buf, dst_ref=off_in.at[d], send_sem=off_send.at[d], recv_sem=off_recv.at[d],
            device_id={"tm": lax.rem(pos + n - 1 - d, n)}, device_id_type=MESH,
        )

    for d in range(n - 1):
        @pl.when(pos - 1 - d >= 0)
        def _(d=d):
            send_off(d).start()

    obs_rows = [at(obs, i) for i in range(WORD)]
    mask_rows = [at(mask, i) for i in range(WORD)]
    errors = jnp.concatenate(obs_rows, axis=0) - times(prior[...], stacked(readout))
    seen = jnp.concatenate(mask_rows, axis=0)
    squares = jnp.sum(seen * active * errors * errors, axis=0, keepdims=True)
    number = jnp.sum(seen, axis=0, keepdims=True)
    sums = jnp.where(row8 == 0, jnp.broadcast_to(squares, (8, states)), jnp.broadcast_to(number, (8, states)))
    sum_buf[...] = sums

    def send_sum(d):
        return pltpu.make_async_remote_copy(
            src_ref=sum_buf, dst_ref=sum_in.at[d], send_sem=sum_send.at[d], recv_sem=sum_recv.at[d],
            device_id={"tm": lax.rem(pos + d + 1, n)}, device_id_type=MESH,
        )

    for d in range(n - 1):
        send_sum(d).start()

    ups = [ends]
    for level in range(levels):
        pair = ups[-1].reshape(ups[-1].shape[0] // 2, 2, 8, states)
        half = pair.shape[0]
        later = times(pair[:, 1].reshape(half * 8, states), power_of(1 << level))
        ups.append(pair[:, 0] + later.reshape(half, 8, states))
    x = jnp.zeros((1, 8, states), F32)
    for level in range(levels - 1, -1, -1):
        count = x.shape[0]
        pair = ups[level].reshape(count, 2, 8, states)
        if level == levels - 1:
            sooner = pair[:, 1]
        else:
            moved = times(x.reshape(count * 8, states), power_of(1 << level))
            sooner = moved.reshape(count, 8, states) + pair[:, 1]
        x = jnp.stack([sooner, x], axis=1).reshape(2 * count, 8, states)
    chunk8[...] = x.reshape(chunks * 8, states)

    for d in range(n - 1):
        @pl.when(pos + 1 + d < n)
        def _(d=d):
            send_off(d).wait_recv()

    left = jnp.concatenate([twice(stacked(off_in[d])) for d in range(1, n - 1)], axis=1)
    x = jnp.where(pos == n - 1, final, off_in[0] + product(left, lap_rhs[...]))
    y = times(x, power_cols[...])
    for k in range(chunks):
        chunk8[k * 8 : (k + 1) * 8, :] += y[:, k * states : (k + 1) * states]
    x = jnp.concatenate([chunk8[pl.ds(b, chunks, stride=8), :] for b in range(seqs)], axis=0)
    y = times(x, fill_rhs)
    for i in range(WORD):
        out[pl.ds(i, total, stride=WORD), :] = (
            suffix[i * total : (i + 1) * total, :] + y[:, i * states : (i + 1) * states]
        )

    for d in range(n - 1):
        send_sum(d).wait_recv()
        sums = sums + sum_in[d]
    squares, number = sums[0:1], sums[1:2]
    grad = 0.5 * active * (number - weight * squares)
    new_prec[...] = log_prec[...] + grad / (seqs * steps * n)
    terms = 0.5 * active * (log_prec[...] * number - weight * squares)
    loglik[...] = jnp.sum(terms, axis=1, keepdims=True) / (seqs * steps * n * states)

    @pl.when(pos < n - 1)
    def _():
        chain.wait_send()

    for d in range(n - 1):
        @pl.when(pos - 1 - d >= 0)
        def _(d=d):
            send_off(d).wait_send()
        send_sum(d).wait_send()


def local(n, obs, present, sensors, log_prec, dynamics, prior_var, obs_map, init_state):
    seqs, steps, channels = obs.shape
    states = dynamics.shape[0]
    chunks = steps // WORD
    total = seqs * chunks
    inner = sum(total >> level for level in range(1, int(math.log2(chunks)) + 1))
    vmem = pl.BlockSpec(memory_space=pltpu.VMEM)
    smem = pl.BlockSpec(memory_space=pltpu.SMEM)
    rows = seqs * steps
    smoothed, new_prec, loglik = pl.pallas_call(
        functools.partial(kernel, n, seqs, steps),
        out_shape=(
            jax.ShapeDtypeStruct((rows, states), F32),
            jax.ShapeDtypeStruct((1, channels), F32),
            jax.ShapeDtypeStruct((1, 1), F32),
        ),
        in_specs=[smem, smem] + [vmem] * 7,
        out_specs=(vmem, vmem, vmem),
        scratch_shapes=[
            pltpu.SMEM((total,), jnp.int32),
            pltpu.VMEM((2**WORD, 2 * states, states), BF16),
            pltpu.VMEM((inner, 2 * states, states), BF16),
            pltpu.VMEM(((inner + 7) // 8 * 8, states), F32),
            pltpu.VMEM((total, states), F32),
            pltpu.VMEM((seqs * 2 * states, chunks * states), BF16),
            pltpu.VMEM((total, states), F32),
            pltpu.VMEM((chunks * 2 * states, states), BF16),
            pltpu.VMEM((2 * states, chunks * states), BF16),
            pltpu.VMEM(((n - 2) * 2 * states, states), BF16),
            pltpu.VMEM((2 * states, 4 * states), BF16),
            pltpu.VMEM((2 * states, 2 * states), BF16),
            pltpu.VMEM((rows, states), F32),
            pltpu.VMEM((rows, states), F32),
            pltpu.VMEM((total, states), F32),
            pltpu.VMEM((rows, states), F32),
            pltpu.VMEM((rows, states), F32),
            pltpu.VMEM((rows, states), F32),
            pltpu.VMEM((chunks * 8, states), F32),
            pltpu.VMEM((8, states), F32),
            pltpu.VMEM((8, states), F32),
            pltpu.VMEM((8, states), F32),
            pltpu.VMEM((n, 8, states), F32),
            pltpu.VMEM((8, states), F32),
            pltpu.VMEM((n, 8, states), F32),
            pltpu.SemaphoreType.DMA((2,)),
            pltpu.SemaphoreType.DMA((n,)),
            pltpu.SemaphoreType.DMA((n,)),
            pltpu.SemaphoreType.DMA((n,)),
            pltpu.SemaphoreType.DMA((n,)),
        ],
        compiler_params=pltpu.CompilerParams(collective_id=0, has_side_effects=True),
        name="kalman",
    )(
        present, sensors, obs.reshape(rows, channels), present, log_prec.reshape(1, channels),
        dynamics, prior_var.reshape(1, states), obs_map, init_state,
    )
    return smoothed.reshape(seqs, steps, states), new_prec.reshape(channels), loglik.reshape(1)


def solution(mesh):
    in_specs = (
        P("cluster", "tm", None),
        P("cluster", "tm"),
        P("cluster"),
        P("cluster"),
        P("cluster", None),
        P("cluster"),
        P("cluster", None),
        P("cluster", None),
    )
    out_specs = (P("cluster", "tm", None), P("cluster"), P("cluster"))
    body = functools.partial(local, mesh.shape["tm"])
    return jax.shard_map(body, mesh=mesh, in_specs=in_specs, out_specs=out_specs, check_vma=False)
```
